1024 devices in a mesh: dp: 32 (over z, core), expert: 32 (over y, x).
Axes of the slice: x: 4, y: 8, z: 16, core: 2. Of those that a mesh axis runs over, the one named last changes fastest.
Arguments:
- tokens: bfloat16 [65536, 1024], P(('dp', 'expert')), may hold values from -6 to 6
- expert_ids: int32 [65536, 8], P(('dp', 'expert')), may hold values from 0 to 63, all different within a row; in each aligned block of 64 rows (0 to 63, 64 to 127, ...) at most 12 rows name the same one
- gates: float32 [65536, 8], P(('dp', 'expert')), may hold values from 0.1 to 0.4
- w_in: bfloat16 [64, 1024, 768], P('expert', 'dp'), may hold values from -0.1875 to 0.1875
- w_out: bfloat16 [64, 384, 1024], P('expert', None, 'dp'), may hold values from -0.3125 to 0.3125
Outputs:
- mixed: bfloat16 [65536, 1024], P(('dp', 'expert'))
The draws below stay inside these ranges and needn't reach their ends.
Inputs may be any that keep to these rules, and one draw needn't show every extreme that they name: `expert_ids`: each row names 8 different experts. Among the 64 rows of one device (aligned blocks), no expert is named by more than 12 rows, a bound that some block reaches.
All inputs are finite; a program needn't handle non-finite values.
Results may differ from the reference program's by a relative error of at most 0.0058.
Values may be sent and summed in bfloat16 or wider, within the bound.
No kernel may reach another device: no remote copies, remote signals or barrier semaphores. Data moves between devices by JAX's collectives and lax.ppermute only.
A program may use at most 32 MiB of HBM per device.

```python
import math
import jax
import jax.numpy as jnp
import numpy as np
from jax import lax

D = 1024
FF = 384
TOPK = 8
TOK_DEV = 64
EXPERTS = 64
TOKENS = 65536
CAP = 12


def level_of(stream_key, shape, cuts, smallest, largest):
    factor_of = 1.0
    for dim, parts in cuts:
        heights = jax.random.uniform(jax.random.fold_in(jax.random.fold_in(stream_key, 6), dim), (parts,), jnp.float32, smallest / len(cuts), largest / len(cuts))
        factor_of = factor_of * jnp.repeat(jnp.exp(heights), shape[dim] // parts).reshape((-1,) + (1,) * (len(shape) - 1 - dim))
    return factor_of


def routed_block(own_key, own, number, rows, amount, top, most, slope):
    sequence = jax.random.permutation(own_key, amount)
    heavy_load, common = load_shares(amount, rows * top, most, slope, True), load_shares(amount, rows * top, most, slope, False)
    places = jnp.arange(amount)

    def named(sizes, turn):
        used = int((sizes > 0).sum())
        fixed = max(1, used // 4)
        moved = fixed + (places - fixed + turn * (used - fixed)) % max(1, amount - fixed)
        return jnp.zeros((amount,), jnp.int32).at[sequence[jnp.where(places < fixed, places, moved)]].set(jnp.asarray(sizes, jnp.int32))

    sizes = jnp.where(number % 4 == 0, named(heavy_load, number // 4), named(common, number - number // 4 - 1))
    mixed = jax.random.permutation(jax.random.fold_in(own, 3), amount)
    donor, taker = mixed[0:amount // 2 * 2:2], mixed[1:amount // 2 * 2:2]
    margin = jnp.minimum(sizes[donor] - 1, most - sizes[taker]) // 2
    margin = jnp.where((donor == sequence[0]) | (taker == sequence[0]) | (sizes[taker] == 0), 0, jnp.maximum(margin, 0))
    moved = jax.random.randint(jax.random.fold_in(own, 4), (amount // 2,), 0, 1 << 20) % (margin + 1)
    sizes = sizes.at[donor].add(-moved).at[taker].add(moved)
    members = jnp.searchsorted(jnp.cumsum(sizes), jnp.arange(rows * top), side="right").astype(jnp.int32)
    listing = members.reshape(top, rows).T
    listing = listing[jax.random.permutation(jax.random.fold_in(own, 1), rows)]
    turn = jax.random.randint(jax.random.fold_in(own, 2), (rows, 1), 0, top)
    return jnp.take_along_axis(listing, (jnp.arange(top)[None, :] + turn) % top, axis=1)


def load_shares(count, total, reach, lean, full):
    weights = [(1 << 20) // math.isqrt(standing ** lean) + 1 for standing in range(1, count + 1)]
    largest = reach if full else min(reach, max(-(-total // count), total * weights[0] // sum(weights)))
    least = 1 if total - largest >= count - 1 else 0
    counts, surplus = [largest] + [least] * (count - 1), total - largest - least * (count - 1)
    while surplus > 0:
        candidates = [i for i in range(1, count) if counts[i] < largest] or [i for i in range(1, count) if counts[i] < reach]
        whole, remaining = sum([weights[i] for i in candidates]), surplus
        for i in candidates:
            addition = min(reach - counts[i], max(1, remaining * weights[i] // whole), surplus)
            counts[i] = counts[i] + addition
            surplus = surplus - addition
    return np.array(counts)


def bell_draw(rng, shape, scale, reach, shards=(), held_as=jnp.bfloat16):
    result = jax.random.normal(rng, shape, jnp.float32) * scale
    if len(shards) > 0:
        result = level_of(rng, shape, shards, -0.22, 0.18) * result
    return jnp.clip(result, min=-reach, max=reach).astype(held_as)


def setup_inputs(seed: int = 0) -> dict:
    splits = jax.random.split(jax.random.key(seed), 6)
    tokens = bell_draw(splits[0], (TOKENS, D), 1.0, 6.0, ((0, 1024),))
    expert_ids_keys = jax.random.split(jax.random.fold_in(splits[1], 1), TOKENS // TOK_DEV)
    expert_ids_turns = jax.random.permutation(jax.random.fold_in(splits[1], 3), TOKENS // TOK_DEV)
    expert_ids = jax.vmap(lambda own, number: routed_block(jax.random.fold_in(splits[1], 2), own, number, TOK_DEV, EXPERTS, TOPK, CAP, 2))(expert_ids_keys, expert_ids_turns).reshape((TOKENS, TOPK))
    gates = jnp.clip(0.1 + 0.3 * jax.random.uniform(splits[2], (TOKENS, TOPK), jnp.float32) ** level_of(splits[2], (TOKENS, TOPK), ((0, 1024),), -0.2, 0.2), 0.1, 0.4)
    w_in = bell_draw(splits[3], (EXPERTS, D, 2 * FF), D ** -0.5, 0.1875, ((0, 32), (1, 32)))
    w_out = bell_draw(splits[4], (EXPERTS, FF, D), FF ** -0.5, 0.3125, ((0, 32), (2, 32)))
    return dict(tokens=tokens, expert_ids=expert_ids, gates=gates, w_in=w_in, w_out=w_out)


def slot_index(expert_ids, experts, capacity):
    flat_ids = expert_ids.reshape(-1)
    onehot = (flat_ids[:, None] == jnp.arange(experts, dtype=jnp.int32)[None, :]).astype(jnp.int32)
    before = jnp.cumsum(onehot, axis=0) - onehot
    position = jnp.sum(before * onehot, axis=1)
    return (flat_ids * capacity + position).astype(jnp.int32)


def reference(tokens, expert_ids, gates, w_in, w_out):
    weights_in = w_in.astype(jnp.float32)
    weights_out = w_out.astype(jnp.float32)
    blocks = TOKENS // TOK_DEV

    def one_block(operands):
        token_rows, route_ids, route_gates = operands
        placed = slot_index(route_ids, EXPERTS, CAP)
        copies = jnp.repeat(token_rows, TOPK, axis=0)
        buffer_rows = jnp.zeros((EXPERTS * CAP, D), token_rows.dtype).at[placed].set(copies)
        grouped = buffer_rows.reshape(EXPERTS, CAP, D).astype(jnp.float32)
        joint_rows = jnp.einsum("ecd,edf->ecf", grouped, weights_in)
        activated = (jax.nn.silu(joint_rows[..., :FF]) * joint_rows[..., FF:]).astype(jnp.bfloat16)
        produced = jnp.einsum("ecf,efd->ecd", activated.astype(jnp.float32), weights_out).astype(jnp.bfloat16)
        picked = produced.reshape(EXPERTS * CAP, D)[placed].reshape(TOK_DEV, TOPK, D).astype(jnp.float32)
        return jnp.sum(route_gates[:, :, None] * picked, axis=1).astype(jnp.bfloat16)

    mixed = lax.map(one_block, (tokens.reshape(blocks, TOK_DEV, D), expert_ids.reshape(blocks, TOK_DEV, TOPK), gates.reshape(blocks, TOK_DEV, TOPK)))
    return mixed.reshape(TOKENS, D)
```

```python
import functools

import jax
import jax.numpy as jnp
from jax import lax
from jax.experimental import pallas as pl
from jax.experimental.pallas import tpu as pltpu
from jax.sharding import Mesh
from jax.sharding import PartitionSpec as P

BF16 = jnp.bfloat16
F32 = jnp.float32
DP = ("z", "c")
ALL = ("z", "c", "expert")
ROWS = 24
BLOCK = 32


def iota(shape, dim):
    return lax.broadcasted_iota(jnp.int32, shape, dim)


def which_expert(q):
    return jnp.where((q >= 20) | ((q >= 8) & (q < 16)), 1, 0)


def which_slot(q):
    return jnp.where(q < 8, q, jnp.where(q < 20, q - 8, q - 12))


def dot(a, b):
    return jnp.dot(a, b, preferred_element_type=F32)


def dot_t(a, b):
    return lax.dot_general(a, b, (((1,), (1,)), ((), ())), preferred_element_type=F32)


def half_order(transposed):
    shape = (256, 256)
    j, k = iota(shape, 1 if transposed else 0), iota(shape, 0 if transposed else 1)
    goes_to = ((j // BLOCK) % 2) * 128 + (j // (2 * BLOCK)) * BLOCK + j % BLOCK
    return (goes_to == k).astype(F32).astype(BF16)


def places(ids, experts):
    rows, top = ids.shape
    lane = iota((rows, experts), 1)
    routed = jnp.zeros((rows, experts), F32)
    for k in range(top):
        routed = routed + (ids[:, k : k + 1] == lane).astype(F32)
    earlier = (iota((rows, rows), 1) < iota((rows, rows), 0)).astype(F32).astype(BF16)
    before = dot(earlier, routed.astype(BF16))
    return jnp.where(routed > 0, before + 1.0, 0.0)


def pack_kernel(ids_ref, tok_ref, out_ref):
    owners, per, width = out_ref.shape
    rows, experts = ids_ref.shape[0], 2 * owners
    place = places(ids_ref[...], experts)
    shape = (owners, per, experts)
    dst, q, lane = iota(shape, 0), iota(shape, 1), iota(shape, 2)
    named = (2 * dst + which_expert(q) == lane).astype(F32).astype(BF16)
    found = dot_t(named.reshape(owners * per, experts), place.astype(BF16))
    shape = (owners, per, rows)
    slot = (which_slot(iota(shape, 1)) + 1).astype(F32).reshape(owners * per, rows)
    pick = (found == slot).astype(F32).astype(BF16)
    order = half_order(False)
    for g in range(width // 256):
        cols = dot(tok_ref[:, g * 256 : (g + 1) * 256], order).astype(BF16)
        for h in range(2):
            placed = dot(pick, cols[:, h * 128 : (h + 1) * 128]).astype(BF16)
            at = h * (width // 2) + g * 128
            out_ref[:, :, at : at + 128] = placed.reshape(owners, per, 128)


def gate_kernel(owners, per, ids_ref, gates_ref, high_ref, low_ref):
    rows, top = ids_ref.shape
    experts = 2 * owners
    ids, gates = ids_ref[...], gates_ref[...]
    place = places(ids, experts)
    lane = iota((rows, experts), 1)
    spread = jnp.zeros((rows, experts), F32)
    for k in range(top):
        spread = spread + jnp.where(ids[:, k : k + 1] == lane, gates[:, k : k + 1], 0.0)
    shape = (owners, per, experts)
    dst, q, lane = iota(shape, 0), iota(shape, 1), iota(shape, 2)
    named = (2 * dst + which_expert(q) == lane).astype(F32).astype(BF16)
    named = named.reshape(owners * per, experts)
    found = dot_t(place.astype(BF16), named)
    q = iota((rows, owners * per), 1) % per
    here = found == (which_slot(q) + 1).astype(F32)
    high = spread.astype(BF16)
    low = (spread - high.astype(F32)).astype(BF16)
    high_ref[...] = jnp.where(here, dot_t(high, named), 0.0).astype(BF16)
    low_ref[...] = jnp.where(here, dot_t(low, named), 0.0).astype(BF16)


def expert_kernel(core_ref, x_ref, a_own, a_other, b_own, b_other, o_own, o_other, y_ref):
    owners, per, width = x_ref.shape
    half = width // 2
    hidden = o_own.shape[-1]
    core = core_ref[0]
    own = pl.ds(pl.multiple_of(core * half, half), half)
    other = pl.ds(pl.multiple_of((1 - core) * half, half), half)
    results = []
    for e, (w_own, w_other) in enumerate(((a_own, a_other), (b_own, b_other))):
        parts = []
        for at in (own, other):
            full = x_ref[:, e * 8 : e * 8 + 8, at].reshape(owners * 8, half)
            rest = x_ref[:, 16:24, at].reshape(owners * 8, half)
            parts.append(jnp.concatenate([full, rest], axis=0))
        joint = dot(parts[0], w_own[...].reshape(half, 2 * hidden))
        joint = joint + dot(parts[1], w_other[...].reshape(half, 2 * hidden))
        gate, up = joint[:, :hidden], joint[:, hidden:]
        activated = (gate * jax.nn.sigmoid(gate) * up).astype(BF16)
        made = []
        for w in (o_own, o_other):
            made.append(dot_t(activated, w[:, e].reshape(half, hidden)))
        results.append(made)
    shape = (owners, 8, half)
    first = iota(shape, 1) < 4
    for at, ya, yb in ((own, results[0][0], results[1][0]), (other, results[0][1], results[1][1])):
        n = owners * 8
        y_ref[:, 0:8, at] = ya[:n].reshape(shape).astype(BF16)
        y_ref[:, 8:16, at] = yb[:n].reshape(shape).astype(BF16)
        rest = jnp.where(first, ya[n:].reshape(shape), yb[n:].reshape(shape))
        y_ref[:, 16:24, at] = rest.astype(BF16)


def combine_kernel(high_ref, low_ref, back_ref, out_ref):
    owners, per, width = back_ref.shape
    back = back_ref[...].reshape(owners * per, width)
    mixed = dot(high_ref[...], back) + dot(low_ref[...], back)
    mixed = mixed.astype(BF16)
    order = half_order(True)
    for g in range(width // 256):
        at = g * 128
        halves = [mixed[:, at : at + 128], mixed[:, width // 2 + at : width // 2 + at + 128]]
        cols = dot(jnp.concatenate(halves, axis=1), order)
        out_ref[:, g * 256 : (g + 1) * 256] = cols.astype(BF16)


def call(kernel, outs, args, flops, moved, smem=0):
    vmem = pl.BlockSpec(memory_space=pltpu.VMEM)
    scalar = pl.BlockSpec(memory_space=pltpu.SMEM)
    return pl.pallas_call(
        kernel,
        out_shape=outs,
        in_specs=[scalar] * smem + [vmem] * (len(args) - smem),
        out_specs=jax.tree.map(lambda _: vmem, outs),
        cost_estimate=pl.CostEstimate(flops=flops, bytes_accessed=moved, transcendentals=0),
    )(*args)


def shards(tokens, expert_ids, gates, w_in, w_out):
    rows, width = tokens.shape
    owners = lax.axis_size("expert")
    hidden = w_out.shape[1]
    slots = owners * ROWS
    shape = jax.ShapeDtypeStruct

    w_out_t = jnp.swapaxes(w_out, 1, 2)
    gathered = [lax.all_gather(w, "z", axis=0) for w in (w_in[0], w_in[1], w_out_t)]
    swapped = [lax.ppermute(w, "c", [(0, 1), (1, 0)]) for w in gathered]
    weights = [w for pair in zip(gathered, swapped) for w in pair]

    outgoing = call(
        pack_kernel,
        shape((owners, ROWS, width), BF16),
        (expert_ids, tokens),
        2 * slots * rows * width,
        2 * slots * width,
    )
    arrived = lax.all_to_all(outgoing, "expert", split_axis=0, concat_axis=0, tiled=True)
    high, low = call(
        functools.partial(gate_kernel, owners, ROWS),
        (shape((rows, slots), BF16), shape((rows, slots), BF16)),
        (expert_ids, gates),
        2 * slots * rows * 256,
        4 * slots * rows,
    )
    core = lax.axis_index("c").astype(jnp.int32).reshape(1)
    produced = call(
        expert_kernel,
        shape((owners, ROWS, width), BF16),
        (core, arrived, *weights),
        2 * 1024 * 3 * hidden * width,
        4 * slots * width + 12 * hidden * width,
        smem=1,
    )
    came_back = lax.all_to_all(produced, "expert", split_axis=0, concat_axis=0, tiled=True)
    return call(
        combine_kernel,
        shape((rows, width), BF16),
        (high, low, came_back),
        4 * slots * rows * width,
        2 * slots * width,
    )


def solution(mesh):
    dp = mesh.shape["dp"]
    finer = Mesh(mesh.devices.reshape(dp // 2, 2, mesh.shape["expert"]), ALL)
    in_specs = (P(ALL, None), P(ALL, None), P(ALL, None), P("expert", DP, None), P("expert", None, DP))
    return jax.shard_map(
        shards, mesh=finer, in_specs=in_specs, out_specs=P(ALL, None), check_vma=False
    )
```

```python
import functools

import jax
import jax.numpy as jnp
from jax import lax
from jax.experimental import pallas as pl
from jax.experimental.pallas import tpu as pltpu
from jax.sharding import Mesh
from jax.sharding import PartitionSpec as P


BF16 = jnp.bfloat16
F32 = jnp.float32
DP = ("z", "c")
ALL = ("z", "c", "expert")
ROWS = 24
BLOCK = 32


def iota(shape, dim):
    return lax.broadcasted_iota(jnp.int32, shape, dim)


def which_expert(q):
    return jnp.where((q >= 20) | ((q >= 8) & (q < 16)), 1, 0)


def which_slot(q):
    return jnp.where(q < 8, q, jnp.where(q < 20, q - 8, q - 12))


def dot(a, b):
    return jnp.dot(a, b, preferred_element_type=F32)


def dot_t(a, b):
    return lax.dot_general(a, b, (((1,), (1,)), ((), ())), preferred_element_type=F32)


def half_order(transposed):
    shape = (256, 256)
    j, k = iota(shape, 1 if transposed else 0), iota(shape, 0 if transposed else 1)
    goes_to = ((j // BLOCK) % 2) * 128 + (j // (2 * BLOCK)) * BLOCK + j % BLOCK
    return (goes_to == k).astype(F32).astype(BF16)


def places(ids, experts):
    top, rows = ids.shape
    line = iota((experts, rows), 0)
    routed = jnp.zeros((experts, rows), F32)
    for k in range(top):
        routed = routed + (ids[k : k + 1, :] == line).astype(F32)
    earlier = (iota((rows, rows), 0) < iota((rows, rows), 1)).astype(F32).astype(BF16)
    before = dot(routed.astype(BF16), earlier)
    return jnp.where(routed > 0, before + 1.0, 0.0)


def row_owners(owners, per):
    shape = (owners, per, 2 * owners)
    named = 2 * iota(shape, 0) + which_expert(iota(shape, 1)) == iota(shape, 2)
    return named.astype(F32).astype(BF16).reshape(owners * per, 2 * owners)


def pack_kernel(ids_ref, tok_ref, out_ref):
    owners, per, width = out_ref.shape
    rows = ids_ref.shape[1]
    place = places(ids_ref[...], 2 * owners)
    found = dot(row_owners(owners, per), place.astype(BF16))
    shape = (owners, per, rows)
    slot = (which_slot(iota(shape, 1)) + 1).astype(F32).reshape(owners * per, rows)
    pick = (found == slot).astype(F32).astype(BF16)
    order = half_order(False)
    for g in range(width // 256):
        cols = dot(tok_ref[:, g * 256 : (g + 1) * 256], order).astype(BF16)
        for h in range(2):
            placed = dot(pick, cols[:, h * 128 : (h + 1) * 128]).astype(BF16)
            at = h * (width // 2) + g * 128
            out_ref[:, :, at : at + 128] = placed.reshape(owners, per, 128)


def gate_kernel(owners, per, ids_ref, gates_ref, high_ref, low_ref):
    top, rows = ids_ref.shape
    experts = 2 * owners
    ids, gates = ids_ref[...], gates_ref[...]
    line = iota((experts, rows), 0)
    spread = jnp.zeros((experts, rows), F32)
    for k in range(top):
        spread = spread + jnp.where(ids[k : k + 1, :] == line, gates[k : k + 1, :], 0.0)
    named = row_owners(owners, per)
    found = dot(named, places(ids, experts).astype(BF16))
    shape = (owners, per, rows)
    slot = (which_slot(iota(shape, 1)) + 1).astype(F32).reshape(owners * per, rows)
    here = found == slot
    high = spread.astype(BF16)
    low = (spread - high.astype(F32)).astype(BF16)
    high_ref[...] = jnp.where(here, dot(named, high), 0.0).astype(BF16).T
    low_ref[...] = jnp.where(here, dot(named, low), 0.0).astype(BF16).T


def assemble_kernel(table_ref, *refs):
    *blocks, out_ref, sems = refs
    copies = []
    for k, block in enumerate(blocks):
        copies.append(pltpu.make_async_copy(block, out_ref.at[table_ref[k]], sems.at[k]))
    for copy in copies:
        copy.start()
    for copy in copies:
        copy.wait()


def expert_kernel(core_ref, x_ref, own_ref, other_ref, y_ref):
    owners, _, width = x_ref.shape
    half = width // 2
    hidden = own_ref.shape[-1] // 3
    core = core_ref[0]
    own = pl.ds(pl.multiple_of(core * half, half), half)
    other = pl.ds(pl.multiple_of((1 - core) * half, half), half)
    sides = ((own, own_ref), (other, other_ref))
    results = []
    for e in range(2):
        joint = 0.0
        for at, w_ref in sides:
            full = x_ref[:, e * 8 : e * 8 + 8, at].reshape(owners * 8, half)
            rest = x_ref[:, 16:24, at].reshape(owners * 8, half)
            part = jnp.concatenate([full, rest], axis=0)
            joint = joint + dot(part, w_ref[:, e, :, : 2 * hidden].reshape(half, 2 * hidden))
        gate, up = joint[:, :hidden], joint[:, hidden:]
        activated = (gate * jax.nn.sigmoid(gate) * up).astype(BF16)
        results.append(
            [dot_t(activated, w_ref[:, e, :, 2 * hidden :].reshape(half, hidden)) for _, w_ref in sides]
        )
    shape = (owners, 8, half)
    first = iota(shape, 1) < 4
    n = owners * 8
    for (at, _), ya, yb in zip(sides, results[0], results[1]):
        y_ref[:, 0:8, at] = ya[:n].reshape(shape).astype(BF16)
        y_ref[:, 8:16, at] = yb[:n].reshape(shape).astype(BF16)
        rest = jnp.where(first, ya[n:].reshape(shape), yb[n:].reshape(shape))
        y_ref[:, 16:24, at] = rest.astype(BF16)


def combine_kernel(high_ref, low_ref, back_ref, out_ref):
    owners, per, width = back_ref.shape
    back = back_ref[...].reshape(owners * per, width)
    mixed = dot(high_ref[...], back) + dot(low_ref[...], back)
    mixed = mixed.astype(BF16)
    order = half_order(True)
    for g in range(width // 256):
        at = g * 128
        halves = [mixed[:, at : at + 128], mixed[:, width // 2 + at : width // 2 + at + 128]]
        cols = dot(jnp.concatenate(halves, axis=1), order)
        out_ref[:, g * 256 : (g + 1) * 256] = cols.astype(BF16)


def call(kernel, outs, args, flops, moved, smem=0):
    vmem = pl.BlockSpec(memory_space=pltpu.VMEM)
    scalar = pl.BlockSpec(memory_space=pltpu.SMEM)
    return pl.pallas_call(
        kernel,
        out_shape=outs,
        in_specs=[scalar] * smem + [vmem] * (len(args) - smem),
        out_specs=jax.tree.map(lambda _: vmem, outs),
        cost_estimate=pl.CostEstimate(flops=flops, bytes_accessed=moved, transcendentals=0),
    )(*args)


def all_blocks(block):
    count = lax.axis_size("z")

    def moved(x, by):
        return lax.ppermute(x, "z", [(i, (i + by) % count) for i in range(count)])

    held = {0: block}
    far = {1: block, -1: block}
    for step in range(1, count // 4 + 1):
        last = 2 * step == count // 2
        coming = {}
        for way in (1, -1):
            x = far[way][max(0, -way)] if last else far[way]
            coming[way] = moved(x, 2 * way)
        for way in (1, -1):
            held[way * (2 * step - 1)] = moved(far[way], way)
        if last:
            held[2 * step] = jnp.stack([coming[1], coming[-1]])
        else:
            held[2 * step], held[-2 * step] = coming[1], coming[-1]
        far = coming
    return held


def shards(tokens, expert_ids, gates, w_in, w_out):
    rows, width = tokens.shape
    owners = lax.axis_size("expert")
    chips = lax.axis_size("z")
    hidden = w_out.shape[1]
    slots = owners * ROWS
    shape = jax.ShapeDtypeStruct
    ids = expert_ids.T

    block = jnp.concatenate([w_in, jnp.swapaxes(w_out, 1, 2)], axis=2)
    held = all_blocks(block)
    outgoing = call(
        pack_kernel,
        shape((owners, ROWS, width), BF16),
        (ids, tokens),
        2 * slots * rows * width,
        2 * slots * width,
    )
    arrived = lax.all_to_all(outgoing, "expert", split_axis=0, concat_axis=0, tiled=True)
    high, low = call(
        functools.partial(gate_kernel, owners, ROWS),
        (shape((rows, slots), BF16), shape((rows, slots), BF16)),
        (ids, gates.T),
        2 * slots * rows * 256,
        4 * slots * rows,
    )
    distances = sorted(held)
    table = (lax.axis_index("z").astype(jnp.int32) - jnp.array(distances, jnp.int32)) % chips
    anywhere = pl.BlockSpec(memory_space=pl.ANY)
    own = pl.pallas_call(
        assemble_kernel,
        out_shape=shape((chips, *block.shape), BF16),
        in_specs=[pl.BlockSpec(memory_space=pltpu.SMEM)] + [anywhere] * chips,
        out_specs=anywhere,
        scratch_shapes=[pltpu.SemaphoreType.DMA((chips,))],
        cost_estimate=pl.CostEstimate(flops=0, bytes_accessed=4 * chips * block.size, transcendentals=0),
    )(table, *[held[d] for d in distances])
    other = lax.ppermute(own, "c", [(0, 1), (1, 0)])
    core = lax.axis_index("c").astype(jnp.int32).reshape(1)
    produced = call(
        expert_kernel,
        shape((owners, ROWS, width), BF16),
        (core, arrived, own, other),
        2 * 1024 * 3 * hidden * width,
        4 * slots * width + 12 * hidden * width,
        smem=1,
    )
    came_back = lax.all_to_all(produced, "expert", split_axis=0, concat_axis=0, tiled=True)
    return call(
        combine_kernel,
        shape((rows, width), BF16),
        (high, low, came_back),
        4 * slots * rows * width,
        2 * slots * width,
    )


def solution(mesh):
    dp = mesh.shape["dp"]
    finer = Mesh(mesh.devices.reshape(dp // 2, 2, mesh.shape["expert"]), ALL)
    in_specs = (P(ALL, None), P(ALL, None), P(ALL, None), P("expert", DP, None), P("expert", None, DP))
    return jax.shard_map(
        shards, mesh=finer, in_specs=in_specs, out_specs=P(ALL, None), check_vma=False
    )
```

```python
import functools

import jax
import jax.numpy as jnp
from jax import lax
from jax.experimental import pallas as pl
from jax.experimental.pallas import tpu as pltpu
from jax.sharding import Mesh
from jax.sharding import PartitionSpec as P

BF16 = jnp.bfloat16
F32 = jnp.float32
DP = ("z", "c")
ALL = ("z", "c", "expert")
ROWS = 24
BLOCK = 32


def iota(shape, dim):
    return lax.broadcasted_iota(jnp.int32, shape, dim)


def which_expert(q):
    return jnp.where((q >= 20) | ((q >= 8) & (q < 16)), 1, 0)


def which_slot(q):
    return jnp.where(q < 8, q, jnp.where(q < 20, q - 8, q - 12))


def dot(a, b):
    return jnp.dot(a, b, preferred_element_type=F32)


def dot_t(a, b):
    return lax.dot_general(a, b, (((1,), (1,)), ((), ())), preferred_element_type=F32)


def chip_order():
    j, k = iota((256, 256), 0), iota((256, 256), 1)
    goes_to = ((j // BLOCK) % 4) * (2 * BLOCK) + (j // 128) * BLOCK + j % BLOCK
    return (goes_to == k).astype(F32).astype(BF16)


def places(ids, experts):
    top, rows = ids.shape
    line = iota((experts, rows), 0)
    routed = jnp.zeros((experts, rows), F32)
    for k in range(top):
        routed = routed + (ids[k : k + 1, :] == line).astype(F32)
    earlier = (iota((rows, rows), 0) < iota((rows, rows), 1)).astype(F32).astype(BF16)
    before = dot(routed.astype(BF16), earlier)
    return jnp.where(routed > 0, before + 1.0, 0.0)


def row_owners(owners, per):
    shape = (owners, per, 2 * owners)
    named = 2 * iota(shape, 0) + which_expert(iota(shape, 1)) == iota(shape, 2)
    return named.astype(F32).astype(BF16).reshape(owners * per, 2 * owners)


def pack_kernel(ids_ref, tok_ref, out_ref):
    owners, per, width = out_ref.shape
    rows = ids_ref.shape[1]
    place = places(ids_ref[...], 2 * owners)
    found = dot(row_owners(owners, per), place.astype(BF16))
    shape = (owners, per, rows)
    slot = (which_slot(iota(shape, 1)) + 1).astype(F32).reshape(owners * per, rows)
    pick = (found == slot).astype(F32).astype(BF16)
    placed = dot(pick, tok_ref[...]).astype(BF16)
    out_ref[...] = placed.reshape(owners, per, width)


def gate_kernel(owners, per, ids_ref, gates_ref, high_ref, low_ref):
    top, rows = ids_ref.shape
    experts = 2 * owners
    ids, gates = ids_ref[...], gates_ref[...]
    line = iota((experts, rows), 0)
    spread = jnp.zeros((experts, rows), F32)
    for k in range(top):
        spread = spread + jnp.where(ids[k : k + 1, :] == line, gates[k : k + 1, :], 0.0)
    named = row_owners(owners, per)
    found = dot(named, places(ids, experts).astype(BF16))
    shape = (owners, per, rows)
    slot = (which_slot(iota(shape, 1)) + 1).astype(F32).reshape(owners * per, rows)
    here = found == slot
    high = spread.astype(BF16)
    low = (spread - high.astype(F32)).astype(BF16)
    high_ref[...] = jnp.where(here, dot(named, high), 0.0).astype(BF16).T
    low_ref[...] = jnp.where(here, dot(named, low), 0.0).astype(BF16).T


def expert_kernel(core_ref, x_ref, in_ref, own_ref, other_ref, y_ref):
    owners, per, width = x_ref.shape
    half = width // 2
    hidden = own_ref.shape[-1]
    core = core_ref[0]
    own = pl.ds(pl.multiple_of(core * half, half), half)
    other = pl.ds(pl.multiple_of((1 - core) * half, half), half)
    sides = ((own, own_ref), (other, other_ref))
    results = []
    for e in range(2):
        full = x_ref[:, e * 8 : e * 8 + 8, :].reshape(owners * 8, width)
        rest = x_ref[:, 16:24, :].reshape(owners * 8, width)
        rows = jnp.concatenate([full, rest], axis=0)
        joint = dot(rows, in_ref[:, e].reshape(width, 2 * hidden))
        gate, up = joint[:, :hidden], joint[:, hidden:]
        activated = (gate * jax.nn.sigmoid(gate) * up).astype(BF16)
        results.append([dot_t(activated, w_ref[:, e].reshape(half, hidden)) for _, w_ref in sides])
    shape = (owners, 8, half)
    first = iota(shape, 1) < 4
    n = owners * 8
    for (at, _), ya, yb in zip(sides, results[0], results[1]):
        y_ref[:, 0:8, at] = ya[:n].reshape(shape).astype(BF16)
        y_ref[:, 8:16, at] = yb[:n].reshape(shape).astype(BF16)
        rest = jnp.where(first, ya[n:].reshape(shape), yb[n:].reshape(shape))
        y_ref[:, 16:24, at] = rest.astype(BF16)


def combine_kernel(high_ref, low_ref, back_ref, out_ref):
    owners, per, width = back_ref.shape
    back = back_ref[...].reshape(owners * per, width)
    mixed = dot(high_ref[...], back) + dot(low_ref[...], back)
    mixed = mixed.astype(BF16)
    order = chip_order()
    for g in range(width // 256):
        at = g * 128
        halves = [mixed[:, at : at + 128], mixed[:, width // 2 + at : width // 2 + at + 128]]
        cols = dot(jnp.concatenate(halves, axis=1), order)
        out_ref[:, g * 256 : (g + 1) * 256] = cols.astype(BF16)


def call(kernel, outs, args, flops, moved, smem=0):
    vmem = pl.BlockSpec(memory_space=pltpu.VMEM)
    scalar = pl.BlockSpec(memory_space=pltpu.SMEM)
    return pl.pallas_call(
        kernel,
        out_shape=outs,
        in_specs=[scalar] * smem + [vmem] * (len(args) - smem),
        out_specs=jax.tree.map(lambda _: vmem, outs),
        cost_estimate=pl.CostEstimate(flops=flops, bytes_accessed=moved, transcendentals=0),
    )(*args)


def shards(tokens, expert_ids, gates, w_in, w_out):
    rows, width = tokens.shape
    owners = lax.axis_size("expert")
    hidden = w_out.shape[1]
    slots = owners * ROWS
    shape = jax.ShapeDtypeStruct
    ids = expert_ids.T

    whole_in = lax.all_gather(w_in, DP, axis=0)
    outgoing = call(
        pack_kernel,
        shape((owners, ROWS, width), BF16),
        (ids, tokens),
        2 * slots * rows * width,
        2 * slots * width,
    )
    arrived = lax.all_to_all(outgoing, "expert", split_axis=0, concat_axis=0, tiled=True)
    own_out = lax.all_gather(jnp.swapaxes(w_out, 1, 2), "z", axis=0)
    other_out = lax.ppermute(own_out, "c", [(0, 1), (1, 0)])
    high, low = call(
        functools.partial(gate_kernel, owners, ROWS),
        (shape((rows, slots), BF16), shape((rows, slots), BF16)),
        (ids, gates.T),
        2 * slots * rows * 256,
        4 * slots * rows,
    )
    core = lax.axis_index("c").astype(jnp.int32).reshape(1)
    produced = call(
        expert_kernel,
        shape((owners, ROWS, width), BF16),
        (core, arrived, whole_in, own_out, other_out),
        2 * 1024 * 3 * hidden * width,
        4 * slots * width + 12 * hidden * width,
        smem=1,
    )
    produced, high, low = lax.optimization_barrier((produced, high, low))
    came_back = lax.all_to_all(produced, "expert", split_axis=0, concat_axis=0, tiled=True)
    return call(
        combine_kernel,
        shape((rows, width), BF16),
        (high, low, came_back),
        4 * slots * rows * width,
        2 * slots * width,
    )


def solution(mesh):
    dp = mesh.shape["dp"]
    finer = Mesh(mesh.devices.reshape(dp // 2, 2, mesh.shape["expert"]), ALL)
    in_specs = (P(ALL, None), P(ALL, None), P(ALL, None), P("expert", DP, None), P("expert", None, DP))
    return jax.shard_map(
        shards, mesh=finer, in_specs=in_specs, out_specs=P(ALL, None), check_vma=False
    )
```

```python
import functools

import jax
import jax.numpy as jnp
from jax import lax
from jax.experimental import pallas as pl
from jax.experimental.pallas import tpu as pltpu
from jax.sharding import Mesh
from jax.sharding import PartitionSpec as P

BF16 = jnp.bfloat16
F32 = jnp.float32
DP = ("z", "c")
ALL = ("z", "c", "expert")
ROWS = 24
BLOCK = 32


def iota(shape, dim):
    return lax.broadcasted_iota(jnp.int32, shape, dim)


def which_expert(q):
    return jnp.where((q >= 20) | ((q >= 8) & (q < 16)), 1, 0)


def which_slot(q):
    return jnp.where(q < 8, q, jnp.where(q < 20, q - 8, q - 12))


def dot(a, b):
    return jnp.dot(a, b, preferred_element_type=F32)


def dot_t(a, b):
    return lax.dot_general(a, b, (((1,), (1,)), ((), ())), preferred_element_type=F32)


def places(ids, experts):
    top, rows = ids.shape
    line = iota((experts, rows), 0)
    routed = jnp.zeros((experts, rows), F32)
    for k in range(top):
        routed = routed + (ids[k : k + 1, :] == line).astype(F32)
    earlier = (iota((rows, rows), 0) < iota((rows, rows), 1)).astype(F32).astype(BF16)
    before = dot(routed.astype(BF16), earlier)
    return jnp.where(routed > 0, before + 1.0, 0.0)


def row_owners(owners, per):
    shape = (owners, per, 2 * owners)
    named = 2 * iota(shape, 0) + which_expert(iota(shape, 1)) == iota(shape, 2)
    return named.astype(F32).astype(BF16).reshape(owners * per, 2 * owners)


def pack_kernel(ids_ref, tok_ref, out_ref):
    owners, per, width = out_ref.shape
    rows = ids_ref.shape[1]
    place = places(ids_ref[...], 2 * owners)
    found = dot(row_owners(owners, per), place.astype(BF16))
    shape = (owners, per, rows)
    slot = (which_slot(iota(shape, 1)) + 1).astype(F32).reshape(owners * per, rows)
    pick = (found == slot).astype(F32).astype(BF16)
    placed = dot(pick, tok_ref[...]).astype(BF16)
    out_ref[...] = placed.reshape(owners, per, width)


def gate_kernel(owners, per, ids_ref, gates_ref, *weight_refs):
    top, rows = ids_ref.shape
    experts = 2 * owners
    ids, gates = ids_ref[...], gates_ref[...]
    line = iota((experts, rows), 0)
    spread = jnp.zeros((experts, rows), F32)
    for k in range(top):
        spread = spread + jnp.where(ids[k : k + 1, :] == line, gates[k : k + 1, :], 0.0)
    named = row_owners(owners, per)
    found = dot(named, places(ids, experts).astype(BF16))
    shape = (owners, per, rows)
    slot = (which_slot(iota(shape, 1)) + 1).astype(F32).reshape(owners * per, rows)
    here = found == slot
    high = spread.astype(BF16)
    low = (spread - high.astype(F32)).astype(BF16)
    for at, part in enumerate((high, low)):
        full = jnp.where(here, dot(named, part), 0.0).reshape(shape)
        for ref, piece in zip(weight_refs, (full[:, :8], full[:, 8:])):
            n = piece.shape[0] * piece.shape[1]
            ref[at * rows : (at + 1) * rows, :] = piece.reshape(n, rows).astype(BF16).T


def expert_rows(x_ref, start, w_in, w_out):
    owners, per, width = x_ref.shape
    hidden = w_out.shape[1]
    full = x_ref[:, start : start + 8, :].reshape(owners * 8, width)
    rest = x_ref[:, 16:24, :].reshape(owners * 8, width)
    joint = dot(jnp.concatenate([full, rest], axis=0), w_in)
    gate, up = joint[:, :hidden], joint[:, hidden:]
    activated = (gate * jax.nn.sigmoid(gate) * up).astype(BF16)
    made = dot_t(activated, w_out)
    shape = (owners, 8, width)
    return made[: owners * 8].reshape(shape), made[owners * 8 :].reshape(shape)


def first_kernel(x_ref, w_ref, full_ref, rest_ref):
    width, both = x_ref.shape[2], w_ref.shape[2]
    wide = 2 * both // 3
    w_in = w_ref[:, :, :wide].reshape(width, wide)
    w_out = w_ref[:, :, wide:].reshape(width, both - wide)
    full, rest = expert_rows(x_ref, 0, w_in, w_out)
    full_ref[...] = full.astype(BF16)
    rest_ref[...] = rest.astype(BF16)


def second_kernel(core_ref, x_ref, in_own, in_other, out_own, out_other, rest_ref, y_ref, w_in, w_out):
    width = x_ref.shape[2]
    core = core_ref[0]
    for whole, own, other in ((w_in, in_own, in_other), (w_out, out_own, out_other)):
        whole[:, pl.ds(core, 1)] = own[...][:, None]
        whole[:, pl.ds(1 - core, 1)] = other[...][:, None]
    full, rest = expert_rows(
        x_ref, 8, w_in[...].reshape(width, w_in.shape[3]), w_out[...].reshape(width, w_out.shape[3])
    )
    y_ref[:, :8] = full.astype(BF16)
    first = iota(rest.shape, 1) < 4
    y_ref[:, 8:] = jnp.where(first, rest_ref[...].astype(F32), rest).astype(BF16)


def combine_kernel(first_weight, second_weight, first_ref, second_ref, out_ref):
    width = out_ref.shape[1]
    mixed = 0.0
    for weight, back in ((first_weight, first_ref), (second_weight, second_ref)):
        mixed = mixed + dot(weight[...], back[...].reshape(-1, width))
    rows = out_ref.shape[0]
    out_ref[...] = (mixed[:rows] + mixed[rows:]).astype(BF16)


def call(kernel, outs, args, flops, moved, smem=0, scratch=()):
    vmem = pl.BlockSpec(memory_space=pltpu.VMEM)
    scalar = pl.BlockSpec(memory_space=pltpu.SMEM)
    return pl.pallas_call(
        kernel,
        out_shape=outs,
        in_specs=[scalar] * smem + [vmem] * (len(args) - smem),
        out_specs=jax.tree.map(lambda _: vmem, outs),
        scratch_shapes=list(scratch),
        cost_estimate=pl.CostEstimate(flops=flops, bytes_accessed=moved, transcendentals=0),
    )(*args)


def swapped(x):
    return lax.ppermute(x, "c", [(0, 1), (1, 0)])


def exchanged(x):
    return lax.all_to_all(x, "expert", split_axis=0, concat_axis=0, tiled=True)


def shards(tokens, expert_ids, gates, w_in, w_out):
    rows, width = tokens.shape
    owners = lax.axis_size("expert")
    chips = lax.axis_size("z")
    hidden = w_out.shape[1]
    slots = owners * ROWS
    ids = expert_ids.T
    w_out = jnp.swapaxes(w_out, 1, 2)

    def bf16(*shape):
        return jax.ShapeDtypeStruct(shape, BF16)

    first_own = jnp.concatenate([w_in[0], w_out[0]], axis=1)
    first_whole = lax.all_gather(first_own, DP, axis=0)
    outgoing = call(
        pack_kernel,
        bf16(owners, ROWS, width),
        (ids, tokens),
        2 * slots * rows * width,
        2 * slots * width,
    )
    arrived = exchanged(outgoing)
    in_own = lax.all_gather(w_in[1], "z", axis=0)
    in_other = swapped(in_own)
    out_own = lax.all_gather(w_out[1], "z", axis=0)
    out_other = swapped(out_own)
    weights = call(
        functools.partial(gate_kernel, owners, ROWS),
        (bf16(2 * rows, owners * 8), bf16(2 * rows, owners * 16)),
        (ids, gates.T),
        2 * slots * rows * 256,
        4 * slots * rows,
    )
    arrived, in_own, out_own, weights = lax.optimization_barrier(
        (arrived, in_own, out_own, tuple(weights))
    )
    work = 2 * 512 * 3 * hidden * width
    first, rest = call(
        first_kernel,
        (bf16(owners, 8, width), bf16(owners, 8, width)),
        (arrived, first_whole),
        work,
        4 * slots * width + 6 * hidden * width,
    )
    first_back = exchanged(first)
    core = lax.axis_index("c").astype(jnp.int32).reshape(1)
    second = call(
        second_kernel,
        bf16(owners, 16, width),
        (core, arrived, in_own, in_other, out_own, out_other, rest),
        work,
        4 * slots * width + 6 * hidden * width,
        smem=1,
        scratch=[
            pltpu.VMEM((chips, 2, BLOCK, 2 * hidden), BF16),
            pltpu.VMEM((chips, 2, BLOCK, hidden), BF16),
        ],
    )
    second_back = exchanged(second)
    return call(
        combine_kernel,
        bf16(rows, width),
        (*weights, first_back, second_back),
        4 * slots * rows * width,
        2 * slots * width,
    )


def solution(mesh):
    dp = mesh.shape["dp"]
    finer = Mesh(mesh.devices.reshape(dp // 2, 2, mesh.shape["expert"]), ALL)
    in_specs = (P(ALL, None), P(ALL, None), P(ALL, None), P("expert", DP, None), P("expert", None, DP))
    return jax.shard_map(
        shards, mesh=finer, in_specs=in_specs, out_specs=P(ALL, None), check_vma=False
    )
```

```python
import functools

import jax
import jax.numpy as jnp
from jax import lax
from jax.experimental import pallas as pl
from jax.experimental.pallas import tpu as pltpu
from jax.sharding import Mesh
from jax.sharding import PartitionSpec as P


BF16 = jnp.bfloat16
F32 = jnp.float32
DP = ("z", "c")
ALL = ("z", "c", "expert")
ROWS = 24
BLOCK = 32


def iota(shape, dim):
    return lax.broadcasted_iota(jnp.int32, shape, dim)


def which_expert(q):
    return jnp.where((q >= 20) | ((q >= 8) & (q < 16)), 1, 0)


def which_slot(q):
    return jnp.where(q < 8, q, jnp.where(q < 20, q - 8, q - 12))


def dot(a, b):
    return jnp.dot(a, b, preferred_element_type=F32)


def dot_t(a, b):
    return lax.dot_general(a, b, (((1,), (1,)), ((), ())), preferred_element_type=F32)


def places(ids, experts):
    top, rows = ids.shape
    line = iota((experts, rows), 0)
    routed = jnp.zeros((experts, rows), F32)
    for k in range(top):
        routed = routed + (ids[k : k + 1, :] == line).astype(F32)
    earlier = (iota((rows, rows), 0) < iota((rows, rows), 1)).astype(F32).astype(BF16)
    before = dot(routed.astype(BF16), earlier)
    return jnp.where(routed > 0, before + 1.0, 0.0)


def row_owners(owners, per):
    shape = (owners, per, 2 * owners)
    named = 2 * iota(shape, 0) + which_expert(iota(shape, 1)) == iota(shape, 2)
    return named.astype(F32).astype(BF16).reshape(owners * per, 2 * owners)


def pack_kernel(ids_ref, tok_ref, out_ref):
    owners, per, width = out_ref.shape
    rows = ids_ref.shape[1]
    place = places(ids_ref[...], 2 * owners)
    found = dot(row_owners(owners, per), place.astype(BF16))
    shape = (owners, per, rows)
    slot = (which_slot(iota(shape, 1)) + 1).astype(F32).reshape(owners * per, rows)
    pick = (found == slot).astype(F32).astype(BF16)
    placed = dot(pick, tok_ref[...]).astype(BF16)
    out_ref[...] = placed.reshape(owners, per, width)


def gate_kernel(owners, per, ids_ref, gates_ref, weight_ref):
    top, rows = ids_ref.shape
    experts = 2 * owners
    ids, gates = ids_ref[...], gates_ref[...]
    line = iota((experts, rows), 0)
    spread = jnp.zeros((experts, rows), F32)
    for k in range(top):
        spread = spread + jnp.where(ids[k : k + 1, :] == line, gates[k : k + 1, :], 0.0)
    named = row_owners(owners, per)
    found = dot(named, places(ids, experts).astype(BF16))
    shape = (owners, per, rows)
    slot = (which_slot(iota(shape, 1)) + 1).astype(F32).reshape(owners * per, rows)
    here = found == slot
    high = spread.astype(BF16)
    low = (spread - high.astype(F32)).astype(BF16)
    for at, part in enumerate((high, low)):
        weight = jnp.where(here, dot(named, part), 0.0).astype(BF16)
        weight_ref[at * rows : (at + 1) * rows, :] = weight.T


def expert_rows(x_ref, start, w_in, w_out):
    owners, _, width = x_ref.shape
    hidden = w_out.shape[1]
    full = x_ref[:, start : start + 8, :].reshape(owners * 8, width)
    rest = x_ref[:, 16:24, :].reshape(owners * 8, width)
    joint = dot(jnp.concatenate([full, rest], axis=0), w_in)
    gate, up = joint[:, :hidden], joint[:, hidden:]
    activated = (gate * jax.nn.sigmoid(gate) * up).astype(BF16)
    made = dot_t(activated, w_out)
    shape = (owners, 8, width)
    return made[: owners * 8].reshape(shape), made[owners * 8 :].reshape(shape)


def expert_kernel(place_ref, x_ref, *refs):
    *blocks, y_ref, whole, sems = refs
    chips = whole.shape[0]
    width, both = x_ref.shape[2], whole.shape[4]
    z, core = place_ref[0], place_ref[1]
    copies = []

    def put(block, chip, lane):
        copies.append(pltpu.make_async_copy(block, whole.at[chip, lane], sems.at[len(copies)]))

    count = chips // 2
    for k, block in enumerate(blocks):
        distance = k if k <= count else k - count
        lane = core if k <= count else 1 - core
        chip = lax.rem(z + (2 * lane - 1) * distance + chips, chips)
        if len(block.shape) == 3:
            put(block, chip, lane)
        else:
            put(block.at[0], chip, lane)
            put(block.at[1], chip, 1 - lane)
    for copy in copies:
        copy.start()
    for copy in copies:
        copy.wait()
    wide = 2 * both // 3
    made = []
    for e in range(2):
        w_in = whole[:, :, e, :, :wide].reshape(width, wide)
        w_out = whole[:, :, e, :, wide:].reshape(width, both - wide)
        full, rest = expert_rows(x_ref, 8 * e, w_in, w_out)
        y_ref[:, 8 * e : 8 * e + 8] = full.astype(BF16)
        made.append(rest)
    first = iota(made[0].shape, 1) < 4
    y_ref[:, 16:24] = jnp.where(first, made[0], made[1]).astype(BF16)


def combine_kernel(weight_ref, back_ref, out_ref):
    rows, width = out_ref.shape
    mixed = dot(weight_ref[...], back_ref[...].reshape(-1, width))
    out_ref[...] = (mixed[:rows] + mixed[rows:]).astype(BF16)


VMEM = pl.BlockSpec(memory_space=pltpu.VMEM)


def call(kernel, outs, args, flops, moved, specs=None, scratch=()):
    return pl.pallas_call(
        kernel,
        out_shape=outs,
        in_specs=[VMEM] * len(args) if specs is None else specs,
        out_specs=VMEM,
        scratch_shapes=list(scratch),
        cost_estimate=pl.CostEstimate(flops=flops, bytes_accessed=moved, transcendentals=0),
    )(*args)


def swapped(x):
    return lax.ppermute(x, "c", [(0, 1), (1, 0)])


def exchanged(x):
    return lax.all_to_all(x, "expert", split_axis=0, concat_axis=0, tiled=True)


def along(x, by):
    n = lax.axis_size("z")
    pairs = [(2 * i + c, 2 * ((i + (1 - 2 * c) * by) % n) + c) for i in range(n) for c in range(2)]
    return lax.ppermute(x, ("z", "c"), pairs)


def all_blocks(own):
    count = lax.axis_size("z") // 2
    block = jnp.stack([own, swapped(own)])
    held = [block] + [None] * count
    far = block
    for step in range(1, count // 2 + 1):
        coming = along(far if 2 * step < count else far[0], 2)
        held[2 * step - 1] = along(far, 1)
        held[2 * step] = far = coming
    return held + [swapped(held[d]) for d in range(1, count + 1)]


def shards(tokens, expert_ids, gates, w_in, w_out):
    rows, width = tokens.shape
    owners = lax.axis_size("expert")
    chips = lax.axis_size("z")
    hidden = w_out.shape[1]
    slots = owners * ROWS
    ids = expert_ids.T

    def bf16(*shape):
        return jax.ShapeDtypeStruct(shape, BF16)

    blocks = all_blocks(jnp.concatenate([w_in, jnp.swapaxes(w_out, 1, 2)], axis=2))
    outgoing = call(
        pack_kernel,
        bf16(owners, ROWS, width),
        (ids, tokens),
        2 * slots * rows * width,
        2 * slots * width,
    )
    arrived = exchanged(outgoing)
    weight = call(
        functools.partial(gate_kernel, owners, ROWS),
        bf16(2 * rows, slots),
        (ids, gates.T),
        2 * slots * rows * 256,
        4 * slots * rows,
    )
    place = jnp.stack([lax.axis_index("z"), lax.axis_index("c")]).astype(jnp.int32)
    produced = call(
        expert_kernel,
        bf16(owners, ROWS, width),
        (place, arrived, *blocks),
        2 * 1024 * 3 * hidden * width,
        4 * slots * width + 12 * hidden * width,
        specs=[pl.BlockSpec(memory_space=pltpu.SMEM), VMEM]
        + [pl.BlockSpec(memory_space=pl.ANY)] * len(blocks),
        scratch=[
            pltpu.VMEM((chips, 2, 2, BLOCK, 3 * hidden), BF16),
            pltpu.SemaphoreType.DMA((2 * chips,)),
        ],
    )
    produced, weight = lax.optimization_barrier((produced, weight))
    back = exchanged(produced)
    return call(
        combine_kernel,
        bf16(rows, width),
        (weight, back),
        4 * slots * rows * width,
        2 * slots * width,
    )


def solution(mesh):
    dp = mesh.shape["dp"]
    finer = Mesh(mesh.devices.reshape(dp // 2, 2, mesh.shape["expert"]), ALL)
    in_specs = (P(ALL, None), P(ALL, None), P(ALL, None), P("expert", DP, None), P("expert", None, DP))
    return jax.shard_map(
        shards, mesh=finer, in_specs=in_specs, out_specs=P(ALL, None), check_vma=False
    )
```

```python
import functools

import jax
import jax.numpy as jnp
from jax import lax
from jax.experimental import pallas as pl
from jax.experimental.pallas import tpu as pltpu
from jax.sharding import Mesh
from jax.sharding import PartitionSpec as P


BF16 = jnp.bfloat16
F32 = jnp.float32
DP = ("z", "c")
ALL = ("z", "c", "expert")
ROWS = 24
BLOCK = 32


def iota(shape, dim):
    return lax.broadcasted_iota(jnp.int32, shape, dim)


def which_expert(q):
    return jnp.where((q >= 20) | ((q >= 8) & (q < 16)), 1, 0)


def which_slot(q):
    return jnp.where(q < 8, q, jnp.where(q < 20, q - 8, q - 12))


def dot(a, b):
    return jnp.dot(a, b, preferred_element_type=F32)


def dot_t(a, b):
    return lax.dot_general(a, b, (((1,), (1,)), ((), ())), preferred_element_type=F32)


def places(ids, experts):
    top, rows = ids.shape
    line = iota((experts, rows), 0)
    routed = jnp.zeros((experts, rows), F32)
    for k in range(top):
        routed = routed + (ids[k : k + 1, :] == line).astype(F32)
    earlier = (iota((rows, rows), 0) < iota((rows, rows), 1)).astype(F32).astype(BF16)
    before = dot(routed.astype(BF16), earlier)
    return jnp.where(routed > 0, before + 1.0, 0.0)


def row_owners(owners, per):
    shape = (owners, per, 2 * owners)
    named = 2 * iota(shape, 0) + which_expert(iota(shape, 1)) == iota(shape, 2)
    return named.astype(F32).astype(BF16).reshape(owners * per, 2 * owners)


def pack_kernel(ids_ref, tok_ref, out_ref):
    owners, per, width = out_ref.shape
    rows = ids_ref.shape[1]
    place = places(ids_ref[...], 2 * owners)
    found = dot(row_owners(owners, per), place.astype(BF16))
    shape = (owners, per, rows)
    slot = (which_slot(iota(shape, 1)) + 1).astype(F32).reshape(owners * per, rows)
    pick = (found == slot).astype(F32).astype(BF16)
    placed = dot(pick, tok_ref[...]).astype(BF16)
    out_ref[...] = placed.reshape(owners, per, width)


def gate_kernel(owners, per, ids_ref, gates_ref, weight_ref):
    top, rows = ids_ref.shape
    experts = 2 * owners
    ids, gates = ids_ref[...], gates_ref[...]
    line = iota((experts, rows), 0)
    spread = jnp.zeros((experts, rows), F32)
    for k in range(top):
        spread = spread + jnp.where(ids[k : k + 1, :] == line, gates[k : k + 1, :], 0.0)
    named = row_owners(owners, per)
    found = dot(named, places(ids, experts).astype(BF16))
    shape = (owners, per, rows)
    slot = (which_slot(iota(shape, 1)) + 1).astype(F32).reshape(owners * per, rows)
    here = found == slot
    high = spread.astype(BF16)
    low = (spread - high.astype(F32)).astype(BF16)
    for at, part in enumerate((high, low)):
        weight = jnp.where(here, dot(named, part), 0.0).astype(BF16)
        weight_ref[at * rows : (at + 1) * rows, :] = weight.T


def expert_rows(x_ref, start, w_in, w_out):
    owners, _, width = x_ref.shape
    hidden = w_out.shape[1]
    full = x_ref[:, start : start + 8, :].reshape(owners * 8, width)
    rest = x_ref[:, 16:24, :].reshape(owners * 8, width)
    joint = dot(jnp.concatenate([full, rest], axis=0), w_in)
    gate, up = joint[:, :hidden], joint[:, hidden:]
    activated = (gate * jax.nn.sigmoid(gate) * up).astype(BF16)
    made = dot_t(activated, w_out)
    shape = (owners, 8, width)
    return made[: owners * 8].reshape(shape), made[owners * 8 :].reshape(shape)


def expert_kernel(place_ref, x_hbm, *refs):
    *blocks, y_hbm, x_ref, y_ref, whole, sems, row_sems = refs
    chips = whole.shape[1]
    width, both = x_ref.shape[2], whole.shape[4]
    z, core = place_ref[0], place_ref[1]
    copies = [[], []]

    def put(block, chip, lane):
        for e in range(2):
            sem = sems.at[e, len(copies[e])]
            copies[e].append(pltpu.make_async_copy(block.at[e], whole.at[e, chip, lane], sem))

    count = chips // 2
    for k, block in enumerate(blocks):
        distance = k if k <= count else k - count
        lane = core if k <= count else 1 - core
        chip = lax.rem(z + (2 * lane - 1) * distance + chips, chips)
        if len(block.shape) == 3:
            put(block, chip, lane)
        else:
            put(block.at[0], chip, lane)
            put(block.at[1], chip, 1 - lane)
    rows_in = pltpu.make_async_copy(x_hbm, x_ref, row_sems.at[0])
    rows_in.start()
    for e in range(2):
        for copy in copies[e]:
            copy.start()
    rows_in.wait()
    wide = 2 * both // 3
    made, out = [], []
    for e in range(2):
        for copy in copies[e]:
            copy.wait()
        w_in = whole[e, :, :, :, :wide].reshape(width, wide)
        w_out = whole[e, :, :, :, wide:].reshape(width, both - wide)
        full, rest = expert_rows(x_ref, 8 * e, w_in, w_out)
        y_ref[e] = full.astype(BF16)
        out.append(pltpu.make_async_copy(y_ref.at[e], y_hbm.at[:, 8 * e : 8 * e + 8], row_sems.at[1 + e]))
        out[e].start()
        made.append(rest)
    first = iota(made[0].shape, 1) < 4
    y_ref[2] = jnp.where(first, made[0], made[1]).astype(BF16)
    out.append(pltpu.make_async_copy(y_ref.at[2], y_hbm.at[:, 16:24], row_sems.at[3]))
    out[2].start()
    for copy in out:
        copy.wait()


def combine_kernel(weight_ref, back_hbm, out_ref, back_ref, sems):
    rows, width = out_ref.shape
    owners, per, _ = back_ref.shape
    parts = sems.shape[0]
    some = owners // parts
    copies = []
    for k in range(parts):
        at = pl.ds(k * some, some)
        copies.append(pltpu.make_async_copy(back_hbm.at[at], back_ref.at[at], sems.at[k]))
        copies[k].start()
    mixed = 0.0
    for k in range(parts):
        copies[k].wait()
        back = back_ref[k * some : (k + 1) * some].reshape(some * per, width)
        mixed = mixed + dot(weight_ref[:, k * some * per : (k + 1) * some * per], back)
    out_ref[...] = (mixed[:rows] + mixed[rows:]).astype(BF16)


VMEM = pl.BlockSpec(memory_space=pltpu.VMEM)
ANY = pl.BlockSpec(memory_space=pl.ANY)


def call(kernel, outs, args, flops, moved, specs=None, out_specs=VMEM, scratch=(), limit=None):
    return pl.pallas_call(
        kernel,
        out_shape=outs,
        in_specs=[VMEM] * len(args) if specs is None else specs,
        out_specs=out_specs,
        scratch_shapes=list(scratch),
        compiler_params=pltpu.CompilerParams(vmem_limit_bytes=limit),
        cost_estimate=pl.CostEstimate(flops=flops, bytes_accessed=moved, transcendentals=0),
    )(*args)


def swapped(x):
    return lax.ppermute(x, "c", [(0, 1), (1, 0)])


def exchanged(x):
    return lax.all_to_all(x, "expert", split_axis=0, concat_axis=0, tiled=True)


def along(x, by):
    n = lax.axis_size("z")
    pairs = [(2 * i + c, 2 * ((i + (1 - 2 * c) * by) % n) + c) for i in range(n) for c in range(2)]
    return lax.ppermute(x, ("z", "c"), pairs)


def all_blocks(own):
    count = lax.axis_size("z") // 2
    block = jnp.stack([own, swapped(own)])
    held = [block] + [None] * count
    far = block
    for step in range(1, count // 2 + 1):
        coming = along(far if 2 * step < count else far[0], 2)
        held[2 * step - 1] = along(far, 1)
        held[2 * step] = far = coming
    return held + [swapped(held[d]) for d in range(1, count + 1)]


def shards(tokens, expert_ids, gates, w_in, w_out):
    rows, width = tokens.shape
    owners = lax.axis_size("expert")
    chips = lax.axis_size("z")
    hidden = w_out.shape[1]
    slots = owners * ROWS
    ids = expert_ids.T

    def bf16(*shape):
        return jax.ShapeDtypeStruct(shape, BF16)

    blocks = all_blocks(jnp.concatenate([w_in, jnp.swapaxes(w_out, 1, 2)], axis=2))
    outgoing = call(
        pack_kernel,
        bf16(owners, ROWS, width),
        (ids, tokens),
        2 * slots * rows * width,
        2 * slots * width,
    )
    arrived = exchanged(outgoing)
    weight = call(
        functools.partial(gate_kernel, owners, ROWS),
        bf16(2 * rows, slots),
        (ids, gates.T),
        2 * slots * rows * 256,
        4 * slots * rows,
    )
    place = jnp.stack([lax.axis_index("z"), lax.axis_index("c")]).astype(jnp.int32)
    produced = call(
        expert_kernel,
        bf16(owners, ROWS, width),
        (place, arrived, *blocks),
        2 * 1024 * 3 * hidden * width,
        4 * slots * width + 12 * hidden * width,
        specs=[pl.BlockSpec(memory_space=pltpu.SMEM)] + [ANY] * (1 + len(blocks)),
        out_specs=ANY,
        scratch=[
            pltpu.VMEM((owners, ROWS, width), BF16),
            pltpu.VMEM((3, owners, 8, width), BF16),
            pltpu.VMEM((2, chips, 2, BLOCK, 3 * hidden), BF16),
            pltpu.SemaphoreType.DMA((2, 2 * chips)),
            pltpu.SemaphoreType.DMA((4,)),
        ],
        limit=28 << 20,
    )
    produced, weight = lax.optimization_barrier((produced, weight))
    back = exchanged(produced)
    return call(
        combine_kernel,
        bf16(rows, width),
        (weight, back),
        4 * slots * rows * width,
        2 * slots * width,
        specs=[VMEM, ANY],
        scratch=[pltpu.VMEM((owners, ROWS, width), BF16), pltpu.SemaphoreType.DMA((2,))],
        limit=16 << 20,
    )


def solution(mesh):
    dp = mesh.shape["dp"]
    finer = Mesh(mesh.devices.reshape(dp // 2, 2, mesh.shape["expert"]), ALL)
    in_specs = (P(ALL, None), P(ALL, None), P(ALL, None), P("expert", DP, None), P("expert", None, DP))
    return jax.shard_map(
        shards, mesh=finer, in_specs=in_specs, out_specs=P(ALL, None), check_vma=False
    )
```

```python
import functools

import jax
import jax.numpy as jnp
from jax import lax
from jax.experimental import pallas as pl
from jax.experimental.pallas import tpu as pltpu
from jax.sharding import Mesh
from jax.sharding import PartitionSpec as P


BF16 = jnp.bfloat16
F32 = jnp.float32
DP = ("z", "c")
ALL = ("z", "c", "expert")
ROWS = 24
BLOCK = 32


def iota(shape, dim):
    return lax.broadcasted_iota(jnp.int32, shape, dim)


def which_expert(q):
    return jnp.where((q >= 20) | ((q >= 8) & (q < 16)), 1, 0)


def which_slot(q):
    return jnp.where(q < 8, q, jnp.where(q < 20, q - 8, q - 12))


def dot(a, b):
    return jnp.dot(a, b, preferred_element_type=F32)


def dot_t(a, b):
    return lax.dot_general(a, b, (((1,), (1,)), ((), ())), preferred_element_type=F32)


def places(ids, experts):
    top, rows = ids.shape
    line = iota((experts, rows), 0)
    routed = jnp.zeros((experts, rows), F32)
    for k in range(top):
        routed = routed + (ids[k : k + 1, :] == line).astype(F32)
    earlier = (iota((rows, rows), 0) < iota((rows, rows), 1)).astype(F32).astype(BF16)
    before = dot(routed.astype(BF16), earlier)
    return jnp.where(routed > 0, before + 1.0, 0.0)


def row_owners(owners, per):
    shape = (owners, per, 2 * owners)
    named = 2 * iota(shape, 0) + which_expert(iota(shape, 1)) == iota(shape, 2)
    return named.astype(F32).astype(BF16).reshape(owners * per, 2 * owners)


def pack_kernel(ids_ref, tok_ref, out_ref):
    owners, per, width = out_ref.shape
    rows = ids_ref.shape[1]
    place = places(ids_ref[...], 2 * owners)
    found = dot(row_owners(owners, per), place.astype(BF16))
    shape = (owners, per, rows)
    slot = (which_slot(iota(shape, 1)) + 1).astype(F32).reshape(owners * per, rows)
    pick = (found == slot).astype(F32).astype(BF16)
    placed = dot(pick, tok_ref[...]).astype(BF16)
    out_ref[...] = placed.reshape(owners, per, width)


def gate_kernel(owners, per, ids_ref, gates_ref, weight_ref):
    top, rows = ids_ref.shape
    experts = 2 * owners
    ids, gates = ids_ref[...], gates_ref[...]
    line = iota((experts, rows), 0)
    spread = jnp.zeros((experts, rows), F32)
    for k in range(top):
        spread = spread + jnp.where(ids[k : k + 1, :] == line, gates[k : k + 1, :], 0.0)
    named = row_owners(owners, per)
    found = dot(named, places(ids, experts).astype(BF16))
    shape = (owners, per, rows)
    slot = (which_slot(iota(shape, 1)) + 1).astype(F32).reshape(owners * per, rows)
    here = found == slot
    high = spread.astype(BF16)
    low = (spread - high.astype(F32)).astype(BF16)
    for at, part in enumerate((high, low)):
        weight = jnp.where(here, dot(named, part), 0.0).astype(BF16)
        weight_ref[at * rows : (at + 1) * rows, :] = weight.T


def expert_rows(x_ref, start, w_in, w_out):
    owners, _, width = x_ref.shape
    hidden = w_out.shape[1]
    full = x_ref[:, start : start + 8, :].reshape(owners * 8, width)
    rest = x_ref[:, 16:24, :].reshape(owners * 8, width)
    joint = dot(jnp.concatenate([full, rest], axis=0), w_in)
    gate, up = joint[:, :hidden], joint[:, hidden:]
    activated = (gate * jax.nn.sigmoid(gate) * up).astype(BF16)
    made = dot_t(activated, w_out)
    shape = (owners, 8, width)
    return made[: owners * 8].reshape(shape), made[owners * 8 :].reshape(shape)


def expert_kernel(place_ref, x_hbm, *refs):
    *blocks, y_hbm, x_ref, y_ref, whole, sems, row_sems = refs
    chips = whole.shape[1]
    width, both = x_ref.shape[2], whole.shape[4]
    z, core = place_ref[0], place_ref[1]
    copies = [[], []]

    def put(block, chip, lane):
        for e in range(2):
            sem = sems.at[e, len(copies[e])]
            copies[e].append(pltpu.make_async_copy(block.at[e], whole.at[e, chip, lane], sem))

    count = chips // 2
    own, others = blocks[: count + 1], blocks[count + 1 :]
    others = [stack.at[k] for stack in others[:2] for k in range(stack.shape[0])] + others[2:]
    for k, block in enumerate(own + others):
        distance = k if k <= count else k - count
        lane = core if k <= count else 1 - core
        chip = lax.rem(z + (2 * lane - 1) * distance + chips, chips)
        if len(block.shape) == 3:
            put(block, chip, lane)
        else:
            put(block.at[0], chip, lane)
            put(block.at[1], chip, 1 - lane)
    rows_in = pltpu.make_async_copy(x_hbm, x_ref, row_sems.at[0])
    rows_in.start()
    for e in range(2):
        for copy in copies[e]:
            copy.start()
    rows_in.wait()
    wide = 2 * both // 3
    made, out = [], []
    for e in range(2):
        for copy in copies[e]:
            copy.wait()
        w_in = whole[e, :, :, :, :wide].reshape(width, wide)
        w_out = whole[e, :, :, :, wide:].reshape(width, both - wide)
        full, rest = expert_rows(x_ref, 8 * e, w_in, w_out)
        y_ref[e] = full.astype(BF16)
        out.append(pltpu.make_async_copy(y_ref.at[e], y_hbm.at[:, 8 * e : 8 * e + 8], row_sems.at[1 + e]))
        out[e].start()
        made.append(rest)
    first = iota(made[0].shape, 1) < 4
    y_ref[2] = jnp.where(first, made[0], made[1]).astype(BF16)
    out.append(pltpu.make_async_copy(y_ref.at[2], y_hbm.at[:, 16:24], row_sems.at[3]))
    out[2].start()
    for copy in out:
        copy.wait()


def combine_kernel(weight_ref, back_hbm, out_ref, back_ref, sems):
    rows, width = out_ref.shape
    owners, per, _ = back_ref.shape
    parts = sems.shape[0]
    some = owners // parts
    copies = []
    for k in range(parts):
        at = pl.ds(k * some, some)
        copies.append(pltpu.make_async_copy(back_hbm.at[at], back_ref.at[at], sems.at[k]))
        copies[k].start()
    mixed = 0.0
    for k in range(parts):
        copies[k].wait()
        back = back_ref[k * some : (k + 1) * some].reshape(some * per, width)
        mixed = mixed + dot(weight_ref[:, k * some * per : (k + 1) * some * per], back)
    out_ref[...] = (mixed[:rows] + mixed[rows:]).astype(BF16)


VMEM = pl.BlockSpec(memory_space=pltpu.VMEM)
ANY = pl.BlockSpec(memory_space=pl.ANY)


def call(kernel, outs, args, flops, moved, specs=None, out_specs=VMEM, scratch=(), limit=None):
    return pl.pallas_call(
        kernel,
        out_shape=outs,
        in_specs=[VMEM] * len(args) if specs is None else specs,
        out_specs=out_specs,
        scratch_shapes=list(scratch),
        compiler_params=pltpu.CompilerParams(vmem_limit_bytes=limit),
        cost_estimate=pl.CostEstimate(flops=flops, bytes_accessed=moved, transcendentals=0),
    )(*args)


def swapped(x):
    return lax.ppermute(x, "c", [(0, 1), (1, 0)])


def exchanged(x):
    return lax.all_to_all(x, "expert", split_axis=0, concat_axis=0, tiled=True)


def along(x, by):
    n = lax.axis_size("z")
    pairs = [(2 * i + c, 2 * ((i + (1 - 2 * c) * by) % n) + c) for i in range(n) for c in range(2)]
    return lax.ppermute(x, ("z", "c"), pairs)


def all_blocks(own):
    count = lax.axis_size("z") // 2
    block = jnp.stack([own, swapped(own)])
    held = [block] + [None] * count
    far = block
    for step in range(1, count // 2 + 1):
        coming = along(far if 2 * step < count else far[0], 2)
        held[2 * step - 1] = along(far, 1)
        held[2 * step] = far = coming
    first = jnp.stack(held[1:5])
    second = jnp.stack(held[5:7])
    others = [swapped(first), swapped(second)]
    return held + others + [swapped(held[7]), swapped(held[8])]


def shards(tokens, expert_ids, gates, w_in, w_out):
    rows, width = tokens.shape
    owners = lax.axis_size("expert")
    chips = lax.axis_size("z")
    hidden = w_out.shape[1]
    slots = owners * ROWS
    ids = expert_ids.T

    def bf16(*shape):
        return jax.ShapeDtypeStruct(shape, BF16)

    blocks = all_blocks(jnp.concatenate([w_in, jnp.swapaxes(w_out, 1, 2)], axis=2))
    outgoing = call(
        pack_kernel,
        bf16(owners, ROWS, width),
        (ids, tokens),
        2 * slots * rows * width,
        2 * slots * width,
    )
    arrived = exchanged(outgoing)
    weight = call(
        functools.partial(gate_kernel, owners, ROWS),
        bf16(2 * rows, slots),
        (ids, gates.T),
        2 * slots * rows * 256,
        4 * slots * rows,
    )
    place = jnp.stack([lax.axis_index("z"), lax.axis_index("c")]).astype(jnp.int32)
    produced = call(
        expert_kernel,
        bf16(owners, ROWS, width),
        (place, arrived, *blocks),
        2 * 1024 * 3 * hidden * width,
        4 * slots * width + 12 * hidden * width,
        specs=[pl.BlockSpec(memory_space=pltpu.SMEM)] + [ANY] * (1 + len(blocks)),
        out_specs=ANY,
        scratch=[
            pltpu.VMEM((owners, ROWS, width), BF16),
            pltpu.VMEM((3, owners, 8, width), BF16),
            pltpu.VMEM((2, chips, 2, BLOCK, 3 * hidden), BF16),
            pltpu.SemaphoreType.DMA((2, 2 * chips)),
            pltpu.SemaphoreType.DMA((4,)),
        ],
        limit=24 << 20,
    )
    produced, weight = lax.optimization_barrier((produced, weight))
    back = exchanged(produced)
    return call(
        combine_kernel,
        bf16(rows, width),
        (weight, back),
        4 * slots * rows * width,
        2 * slots * width,
        specs=[VMEM, ANY],
        scratch=[pltpu.VMEM((owners, ROWS, width), BF16), pltpu.SemaphoreType.DMA((2,))],
        limit=16 << 20,
    )


def solution(mesh):
    dp = mesh.shape["dp"]
    finer = Mesh(mesh.devices.reshape(dp // 2, 2, mesh.shape["expert"]), ALL)
    in_specs = (P(ALL, None), P(ALL, None), P(ALL, None), P("expert", DP, None), P("expert", None, DP))
    return jax.shard_map(
        shards, mesh=finer, in_specs=in_specs, out_specs=P(ALL, None), check_vma=False
    )
```

```python
import functools

import jax
import jax.numpy as jnp
from jax import lax
from jax.experimental import pallas as pl
from jax.experimental.pallas import tpu as pltpu
from jax.sharding import Mesh
from jax.sharding import PartitionSpec as P


BF16 = jnp.bfloat16
F32 = jnp.float32
DP = ("z", "c")
ALL = ("z", "c", "expert")
ROWS = 24
BLOCK = 32


def iota(shape, dim):
    return lax.broadcasted_iota(jnp.int32, shape, dim)


def which_expert(q):
    return jnp.where((q >= 20) | ((q >= 8) & (q < 16)), 1, 0)


def which_slot(q):
    return jnp.where(q < 8, q, jnp.where(q < 20, q - 8, q - 12))


def dot(a, b):
    return jnp.dot(a, b, preferred_element_type=F32)


def dot_t(a, b):
    return lax.dot_general(a, b, (((1,), (1,)), ((), ())), preferred_element_type=F32)


def places(ids, experts):
    top, rows = ids.shape
    line = iota((experts, rows), 0)
    routed = jnp.zeros((experts, rows), F32)
    for k in range(top):
        routed = routed + (ids[k : k + 1, :] == line).astype(F32)
    earlier = (iota((rows, rows), 0) < iota((rows, rows), 1)).astype(F32).astype(BF16)
    before = dot(routed.astype(BF16), earlier)
    return jnp.where(routed > 0, before + 1.0, 0.0)


def row_owners(owners, per):
    shape = (owners, per, 2 * owners)
    named = 2 * iota(shape, 0) + which_expert(iota(shape, 1)) == iota(shape, 2)
    return named.astype(F32).astype(BF16).reshape(owners * per, 2 * owners)


def pack_kernel(ids_ref, tok_ref, out_ref):
    owners, per, width = out_ref.shape
    rows = ids_ref.shape[1]
    place = places(ids_ref[...], 2 * owners)
    found = dot(row_owners(owners, per), place.astype(BF16))
    shape = (owners, per, rows)
    slot = (which_slot(iota(shape, 1)) + 1).astype(F32).reshape(owners * per, rows)
    pick = (found == slot).astype(F32).astype(BF16)
    placed = dot(pick, tok_ref[...]).astype(BF16)
    out_ref[...] = placed.reshape(owners, per, width)


def gate_kernel(owners, per, ids_ref, gates_ref, weight_ref):
    top, rows = ids_ref.shape
    experts = 2 * owners
    ids, gates = ids_ref[...], gates_ref[...]
    line = iota((experts, rows), 0)
    spread = jnp.zeros((experts, rows), F32)
    for k in range(top):
        spread = spread + jnp.where(ids[k : k + 1, :] == line, gates[k : k + 1, :], 0.0)
    named = row_owners(owners, per)
    found = dot(named, places(ids, experts).astype(BF16))
    shape = (owners, per, rows)
    slot = (which_slot(iota(shape, 1)) + 1).astype(F32).reshape(owners * per, rows)
    here = found == slot
    high = spread.astype(BF16)
    low = (spread - high.astype(F32)).astype(BF16)
    for at, part in enumerate((high, low)):
        weight = jnp.where(here, dot(named, part), 0.0).astype(BF16)
        weight_ref[at * rows : (at + 1) * rows, :] = weight.T


def paired(first, second):
    upper = iota(first.shape, 1) < 4
    return (
        jnp.where(upper, first, pltpu.roll(second, 4, 1)),
        jnp.where(upper, pltpu.roll(first, 4, 1), second),
    )


def expert_rows(full, rest, w_in, w_out):
    hidden = w_out.shape[1]
    count = full.shape[0]
    joint = dot(jnp.concatenate([full, rest], axis=0), w_in)
    gate, up = joint[:, :hidden], joint[:, hidden:]
    activated = (gate * jax.nn.sigmoid(gate) * up).astype(BF16)
    made = dot_t(activated, w_out)
    return made[:count], made[count:]


def expert_kernel(place_ref, x_hbm, *refs):
    *blocks, y_hbm, x_ref, y_ref, whole, sems, row_sems = refs
    chips = whole.shape[1]
    width, both = x_ref.shape[2], whole.shape[4]
    z, core = place_ref[0], place_ref[1]
    copies = [[], []]

    def put(block, chip, lane):
        for e in range(2):
            sem = sems.at[e, len(copies[e])]
            copies[e].append(pltpu.make_async_copy(block.at[e], whole.at[e, chip, lane], sem))

    count = chips // 2
    single = []
    for block in blocks:
        stacked = len(block.shape) == 5
        single += [block.at[k] for k in range(block.shape[0])] if stacked else [block]
    del single[count + 1]
    for k, block in enumerate(single):
        distance = k if k <= count else k - count
        lane = core if k <= count else 1 - core
        chip = lax.rem(z + (2 * lane - 1) * distance + chips, chips)
        if len(block.shape) == 3:
            put(block, chip, lane)
        else:
            put(block.at[0], chip, lane)
            put(block.at[1], chip, 1 - lane)
    rows_in = pltpu.make_async_copy(x_hbm, x_ref, row_sems.at[0])
    rows_in.start()
    for e in range(2):
        for copy in copies[e]:
            copy.start()
    rows_in.wait()
    owners = x_ref.shape[0]
    wide = 2 * both // 3
    made, out = [], []
    rest = x_ref[:, 16:24, :].astype(F32).reshape(owners // 2, 2, 8, width)
    rests = [part.reshape(owners * 4, width).astype(BF16) for part in paired(rest[:, 0], rest[:, 1])]
    for e in range(2):
        for copy in copies[e]:
            copy.wait()
        w_in = whole[e, :, :, :, :wide].reshape(width, wide)
        w_out = whole[e, :, :, :, wide:].reshape(width, both - wide)
        rows = x_ref[:, 8 * e : 8 * e + 8, :].reshape(owners * 8, width)
        full, few = expert_rows(rows, rests[e], w_in, w_out)
        y_ref[e] = full.reshape(owners, 8, width).astype(BF16)
        out.append(pltpu.make_async_copy(y_ref.at[e], y_hbm.at[:, 8 * e : 8 * e + 8], row_sems.at[1 + e]))
        out[e].start()
        made.append(few.reshape(owners // 2, 8, width))
    even, odd = paired(*made)
    y_ref[2] = jnp.stack([even, odd], axis=1).reshape(owners, 8, width).astype(BF16)
    out.append(pltpu.make_async_copy(y_ref.at[2], y_hbm.at[:, 16:24], row_sems.at[3]))
    out[2].start()
    for copy in out:
        copy.wait()


def combine_kernel(weight_ref, back_hbm, out_ref, back_ref, sems):
    rows, width = out_ref.shape
    owners, per, _ = back_ref.shape
    parts = sems.shape[0]
    some = owners // parts
    copies = []
    for k in range(parts):
        at = pl.ds(k * some, some)
        copies.append(pltpu.make_async_copy(back_hbm.at[at], back_ref.at[at], sems.at[k]))
        copies[k].start()
    mixed = 0.0
    for k in range(parts):
        copies[k].wait()
        back = back_ref[k * some : (k + 1) * some].reshape(some * per, width)
        mixed = mixed + dot(weight_ref[:, k * some * per : (k + 1) * some * per], back)
    out_ref[...] = (mixed[:rows] + mixed[rows:]).astype(BF16)


VMEM = pl.BlockSpec(memory_space=pltpu.VMEM)
ANY = pl.BlockSpec(memory_space=pl.ANY)


def call(kernel, outs, args, flops, moved, specs=None, out_specs=VMEM, scratch=(), limit=None):
    return pl.pallas_call(
        kernel,
        out_shape=outs,
        in_specs=[VMEM] * len(args) if specs is None else specs,
        out_specs=out_specs,
        scratch_shapes=list(scratch),
        compiler_params=pltpu.CompilerParams(vmem_limit_bytes=limit),
        cost_estimate=pl.CostEstimate(flops=flops, bytes_accessed=moved, transcendentals=0),
    )(*args)


def swapped(x):
    return lax.ppermute(x, "c", [(0, 1), (1, 0)])


def exchanged(x):
    return lax.all_to_all(x, "expert", split_axis=0, concat_axis=0, tiled=True)


def along(x, by):
    n = lax.axis_size("z")
    pairs = [(2 * i + c, 2 * ((i + (1 - 2 * c) * by) % n) + c) for i in range(n) for c in range(2)]
    return lax.ppermute(x, ("z", "c"), pairs)


def all_blocks(own):
    count = lax.axis_size("z") // 2
    block = jnp.stack([own, swapped(own)])
    held = [block] + [None] * count
    far = block
    for step in range(1, count // 2 + 1):
        coming = along(far if 2 * step < count else far[0], 2)
        held[2 * step - 1] = along(far, 1)
        held[2 * step] = far = coming
    first = jnp.stack(held[0:5])
    second = jnp.stack(held[5:7])
    others = [swapped(first), swapped(second)]
    others += [swapped(held[7]), swapped(held[8])]
    return [first, second, held[7], held[8]] + others


def shards(tokens, expert_ids, gates, w_in, w_out):
    rows, width = tokens.shape
    owners = lax.axis_size("expert")
    chips = lax.axis_size("z")
    hidden = w_out.shape[1]
    slots = owners * ROWS
    ids = expert_ids.T

    def bf16(*shape):
        return jax.ShapeDtypeStruct(shape, BF16)

    blocks = all_blocks(jnp.concatenate([w_in, jnp.swapaxes(w_out, 1, 2)], axis=2))
    outgoing = call(
        pack_kernel,
        bf16(owners, ROWS, width),
        (ids, tokens),
        2 * slots * rows * width,
        2 * slots * width,
    )
    arrived = exchanged(outgoing)
    weight = call(
        functools.partial(gate_kernel, owners, ROWS),
        bf16(2 * rows, slots),
        (ids, gates.T),
        2 * slots * rows * 256,
        4 * slots * rows,
    )
    place = jnp.stack([lax.axis_index("z"), lax.axis_index("c")]).astype(jnp.int32)
    produced = call(
        expert_kernel,
        bf16(owners, ROWS, width),
        (place, arrived, *blocks),
        2 * 1024 * 3 * hidden * width,
        4 * slots * width + 12 * hidden * width,
        specs=[pl.BlockSpec(memory_space=pltpu.SMEM)] + [ANY] * (1 + len(blocks)),
        out_specs=ANY,
        scratch=[
            pltpu.VMEM((owners, ROWS, width), BF16),
            pltpu.VMEM((3, owners, 8, width), BF16),
            pltpu.VMEM((2, chips, 2, BLOCK, 3 * hidden), BF16),
            pltpu.SemaphoreType.DMA((2, 2 * chips)),
            pltpu.SemaphoreType.DMA((4,)),
        ],
        limit=18 << 20,
    )
    produced, weight = lax.optimization_barrier((produced, weight))
    back = exchanged(produced)
    return call(
        combine_kernel,
        bf16(rows, width),
        (weight, back),
        4 * slots * rows * width,
        2 * slots * width,
        specs=[VMEM, ANY],
        scratch=[pltpu.VMEM((owners, ROWS, width), BF16), pltpu.SemaphoreType.DMA((2,))],
        limit=16 << 20,
    )


def solution(mesh):
    dp = mesh.shape["dp"]
    finer = Mesh(mesh.devices.reshape(dp // 2, 2, mesh.shape["expert"]), ALL)
    in_specs = (P(ALL, None), P(ALL, None), P(ALL, None), P("expert", DP, None), P("expert", None, DP))
    return jax.shard_map(
        shards, mesh=finer, in_specs=in_specs, out_specs=P(ALL, None), check_vma=False
    )
```
